32 devices in a mesh: row: 8 (over y, x, core), col: 4 (over z).
Axes of the slice: x: 2, y: 2, z: 4, core: 2. Of those that a mesh axis runs over, the one named last changes fastest.
Arguments:
- matrix: float32 [16384, 16384], P('row', 'col'), may hold values from -80 to 80
Outputs:
- reduced: float32 [16384, 16384], P('row', 'col')
The draws below stay inside these ranges and needn't reach their ends.
All inputs are finite; a program needn't handle non-finite values.
Results may differ from the reference program's by a relative error of at most 0.0003.
Values sent between devices are 32-bit elements; how exact they have to be, the bound alone decides.
A program may use at most 128 MiB of HBM per device.

```python
import jax
import jax.numpy as jnp
from jax import lax

ORDER = 16384
B = 64
PANELS = 1


def draw_matrix(key, part):
    first_key = jax.random.fold_in(key, 11)
    base = jax.random.truncated_normal(first_key, -6.0, 6.0, (ORDER, ORDER), jnp.float32)
    symmetric = (base + base.T) * jnp.float32(0.5 ** 0.5)
    return symmetric


def setup_inputs(seed: int = 0) -> dict:
    key_list = jax.random.split(jax.random.key(seed), 2)
    matrix = draw_matrix(jax.random.fold_in(key_list[1], 71), 0)
    return {"matrix": matrix}


def product(left, right):
    return jnp.dot(left.astype(jnp.float32), right.astype(jnp.float32), precision=lax.Precision.HIGHEST, preferred_element_type=jnp.float32)

def sign_lu(block):
    work = block
    count = block.shape[0]
    unit_lower = jnp.eye(count, dtype=block.dtype)
    signs = []
    for column in range(count):
        pivot = work[column, column]
        sign_value = jnp.where(pivot >= 0, -jnp.ones_like(pivot), jnp.ones_like(pivot))
        work = work.at[column, column].add(-sign_value)
        below = work[column + 1:, column] / work[column, column]
        unit_lower = unit_lower.at[column + 1:, column].set(below)
        work = work.at[column + 1:, column + 1:].add(-below[:, None] * work[column, column + 1:][None, :])
        signs.append(sign_value)
    return (unit_lower, jnp.triu(work), jnp.stack(signs))

def reference(matrix):
    current = matrix
    indices = jnp.arange(ORDER, dtype=jnp.int32)
    identity = jnp.eye(B, dtype=matrix.dtype)
    for panel_index in range(PANELS):
        first = panel_index * B
        limit = first + B
        panel = jnp.where(indices[:, None] >= limit, current[:, first:limit], jnp.zeros_like(current[:, first:limit]))
        gram_matrix = product(panel.T, panel)
        lower_factor = jnp.linalg.cholesky(gram_matrix)
        basis = jax.scipy.linalg.solve_triangular(lower_factor, panel.T, lower=True).T
        top_basis = basis[limit:limit + B]
        unit_lower, upper, signs = sign_lu(top_basis)
        inverse_upper = jax.scipy.linalg.solve_triangular(upper, identity, lower=False)
        inverse_lower = jax.scipy.linalg.solve_triangular(unit_lower, identity, lower=True, unit_diagonal=True)
        factor = -product(upper * signs[None, :], inverse_lower.T)
        shifted = signs[:, None] * inverse_upper
        vectors = product(basis, inverse_upper)
        vectors = vectors.at[limit:limit + B].add(-shifted)
        image = product(current, vectors)
        projected = product(vectors.T, image)
        inner = product(factor.T, product(projected, factor))
        update = product(image, factor) - 0.5 * product(vectors, inner)
        current = current - product(vectors, update.T) - product(update, vectors.T)
    return current
```

```python
import jax
import jax.numpy as jnp
from jax import lax
from jax.experimental import pallas as pl
from jax.experimental.pallas import tpu as pltpu
from jax.sharding import PartitionSpec as P

B = 64


highest = lax.Precision.HIGHEST
high = lax.Precision.HIGH
f32 = jnp.float32


def from_root(x, axis, root):
    mine = lax.axis_index(axis) == root
    return lax.psum(jnp.where(mine, x, jnp.zeros_like(x)), axis)


def product(left, right, precision=highest):
    return jnp.dot(left, right, precision=precision, preferred_element_type=f32)


def product_nt(left, right):
    return lax.dot_general(
        left, right, (((1,), (1,)), ((), ())), precision=highest, preferred_element_type=f32
    )


def factor_values(gram, top):
    rows = lax.broadcasted_iota(jnp.int32, (B, 2 * B), 0)
    lanes = lax.broadcasted_iota(jnp.int32, (B, 2 * B), 1)
    eye = jnp.where(rows + B == lanes, f32(1.0), f32(0.0))
    small_rows = lax.broadcasted_iota(jnp.int32, (B, B), 0)
    small_lanes = lax.broadcasted_iota(jnp.int32, (B, B), 1)
    eye_half = jnp.where(small_rows == small_lanes, f32(1.0), f32(0.0))
    work = jnp.concatenate([gram, eye_half], axis=1)
    for j in range(B):
        inverse = 1.0 / jnp.sqrt(work[j : j + 1, j : j + 1])
        row = work[j : j + 1, :] * inverse
        column = work[:, j : j + 1] * inverse
        lowered = work - column * row
        work = jnp.where(rows > j, lowered, jnp.where(rows == j, row, work))
    lower_inverse = work[:, B:]
    top_basis = product_nt(top, lower_inverse)
    top_turned = product_nt(lower_inverse, top)
    q = jnp.concatenate([top_basis, eye_half], axis=1)
    t = jnp.concatenate([top_turned, eye_half], axis=1)
    signs = jnp.zeros((1, B), f32)
    sign_lane = lax.broadcasted_iota(jnp.int32, (1, B), 1)
    reciprocals = jnp.zeros((B, 1), f32)
    sublane = lax.broadcasted_iota(jnp.int32, (B, 1), 0)
    one_row = lax.broadcasted_iota(jnp.int32, (1, 2 * B), 1)
    for j in range(B):
        pivot = q[j : j + 1, j : j + 1]
        sign = jnp.where(pivot >= 0, f32(-1.0), f32(1.0))
        inverse = 1.0 / (pivot - sign)
        row_q = q[j : j + 1, :] - jnp.where(one_row == j, sign, f32(0.0))
        row_t = t[j : j + 1, :] - jnp.where(one_row == j, sign, f32(0.0))
        below_q = q[:, j : j + 1] * inverse
        below_t = t[:, j : j + 1] * inverse
        q = jnp.where(rows > j, q - below_q * row_q, jnp.where(rows == j, row_q, q))
        t = jnp.where(rows > j, t - below_t * row_t, t)
        signs = jnp.where(sign_lane == j, sign, signs)
        reciprocals = jnp.where(sublane == j, inverse, reciprocals)
    upper = jnp.where(small_lanes >= small_rows, q[:, :B], f32(0.0))
    unit_inverse = q[:, B:]
    upper_inverse_turned = t[:, B:] * reciprocals
    factor = -product_nt(upper * signs, unit_inverse)
    first = product(upper_inverse_turned, lower_inverse)
    second = upper_inverse_turned * signs
    return first, second, factor


def factor_kernel(gram_ref, top_ref, first_ref, second_ref, factor_ref):
    first, second, factor = factor_values(gram_ref[...], top_ref[...])
    first_ref[...] = first
    second_ref[...] = second
    factor_ref[...] = factor


def factors(gram, top):
    vmem = pl.BlockSpec(memory_space=pltpu.VMEM)
    return pl.pallas_call(
        factor_kernel,
        out_shape=[jax.ShapeDtypeStruct((B, B), f32)] * 3,
        in_specs=[vmem] * 2,
        out_specs=[vmem] * 3,
    )(gram, top)


def shards(matrix):
    height, breadth = matrix.shape
    col_index = lax.axis_index("col")
    row_start = lax.axis_index("row") * height
    col_start = col_index * breadth
    global_rows = row_start + jnp.arange(height, dtype=jnp.int32)
    global_cols = col_start + jnp.arange(breadth, dtype=jnp.int32)
    slots = jnp.arange(B, dtype=jnp.int32)
    current = matrix
    limit = B
    column_piece = from_root(current[:, 0:limit], "col", 0)
    panel_rows = jnp.where(global_rows[:, None] >= limit, column_piece, jnp.float32(0.0))
    row_piece = from_root(current[0:limit, :], "row", 0)
    panel_cols = jnp.where(global_cols[None, :] >= limit, row_piece, jnp.float32(0.0))
    onehot_rows = jnp.where(
        global_rows[:, None] - limit == slots[None, :], jnp.float32(1.0), jnp.float32(0.0)
    )
    onehot_cols = jnp.where(
        global_cols[:, None] - limit == slots[None, :], jnp.float32(1.0), jnp.float32(0.0)
    )
    gram_matrix, top_panel = lax.psum(
        (product(panel_rows.T, panel_rows), product(onehot_rows.T, panel_rows)), "row"
    )
    first, second, factor = factors(gram_matrix, top_panel)
    vectors_rows = product(panel_rows, first.T) - product(onehot_rows, second.T)
    vectors_cols = product(first, panel_cols) - product(second, onehot_cols.T)
    image_rows = lax.psum(product(current, vectors_cols.T, high), "col")
    projected = lax.psum(product(vectors_rows.T, image_rows), "row")
    inner = product(factor.T, product(projected, factor))
    update_rows = product(image_rows, factor) - 0.5 * product(vectors_rows, inner)
    image_cols = lax.psum(product(vectors_rows.T, current, high), "row")
    update_cols = product(factor.T, image_cols) - 0.5 * product(inner.T, vectors_cols)
    current = current - product(
        jnp.concatenate([vectors_rows, update_rows], 1), jnp.concatenate([update_cols, vectors_cols], 0), high
    )
    return current


def solution(mesh):
    placed = (P("row", "col"),)
    return jax.shard_map(
        shards, mesh=mesh, in_specs=placed, out_specs=P("row", "col"), check_vma=False
    )
```

```python
import jax
import jax.numpy as jnp
from jax import lax
from jax.experimental import pallas as pl
from jax.experimental.pallas import tpu as pltpu
from jax.sharding import PartitionSpec as P

B = 64


highest = lax.Precision.HIGHEST
MESH = pl.DeviceIdType.MESH
high = lax.Precision.HIGH
f32 = jnp.float32


def product(left, right, precision=highest):
    return jnp.dot(left, right, precision=precision, preferred_element_type=f32)


def product_nt(left, right):
    return lax.dot_general(
        left, right, (((1,), (1,)), ((), ())), precision=highest, preferred_element_type=f32
    )


def factor_values(gram, top):
    rows = lax.broadcasted_iota(jnp.int32, (B, 2 * B), 0)
    lanes = lax.broadcasted_iota(jnp.int32, (B, 2 * B), 1)
    eye = jnp.where(rows + B == lanes, f32(1.0), f32(0.0))
    small_rows = lax.broadcasted_iota(jnp.int32, (B, B), 0)
    small_lanes = lax.broadcasted_iota(jnp.int32, (B, B), 1)
    eye_half = jnp.where(small_rows == small_lanes, f32(1.0), f32(0.0))
    work = jnp.concatenate([gram, eye_half], axis=1)
    for j in range(B):
        inverse = 1.0 / jnp.sqrt(work[j : j + 1, j : j + 1])
        row = work[j : j + 1, :] * inverse
        column = work[:, j : j + 1] * inverse
        lowered = work - column * row
        work = jnp.where(rows > j, lowered, jnp.where(rows == j, row, work))
    lower_inverse = work[:, B:]
    top_basis = product_nt(top, lower_inverse)
    top_turned = product_nt(lower_inverse, top)
    q = jnp.concatenate([top_basis, eye_half], axis=1)
    t = jnp.concatenate([top_turned, eye_half], axis=1)
    signs = jnp.zeros((1, B), f32)
    sign_lane = lax.broadcasted_iota(jnp.int32, (1, B), 1)
    reciprocals = jnp.zeros((B, 1), f32)
    sublane = lax.broadcasted_iota(jnp.int32, (B, 1), 0)
    one_row = lax.broadcasted_iota(jnp.int32, (1, 2 * B), 1)
    for j in range(B):
        pivot = q[j : j + 1, j : j + 1]
        sign = jnp.where(pivot >= 0, f32(-1.0), f32(1.0))
        inverse = 1.0 / (pivot - sign)
        row_q = q[j : j + 1, :] - jnp.where(one_row == j, sign, f32(0.0))
        row_t = t[j : j + 1, :] - jnp.where(one_row == j, sign, f32(0.0))
        below_q = q[:, j : j + 1] * inverse
        below_t = t[:, j : j + 1] * inverse
        q = jnp.where(rows > j, q - below_q * row_q, jnp.where(rows == j, row_q, q))
        t = jnp.where(rows > j, t - below_t * row_t, t)
        signs = jnp.where(sign_lane == j, sign, signs)
        reciprocals = jnp.where(sublane == j, inverse, reciprocals)
    upper = jnp.where(small_lanes >= small_rows, q[:, :B], f32(0.0))
    unit_inverse = q[:, B:]
    upper_inverse_turned = t[:, B:] * reciprocals
    factor = -product_nt(upper * signs, unit_inverse)
    factor_turned = -product_nt(unit_inverse, upper * signs)
    first = product(upper_inverse_turned, lower_inverse)
    second = upper_inverse_turned * signs
    return first, second, factor, factor_turned


def remote(src, dst, send_sem, recv_sem, device):
    return pltpu.make_async_remote_copy(
        src_ref=src,
        dst_ref=dst,
        send_sem=send_sem,
        recv_sem=recv_sem,
        device_id=device,
        device_id_type=MESH,
    )


def greet_all(height, breadth, me_row, me_col):
    count = height * breadth
    me = me_row * breadth + me_col
    barrier = pltpu.get_barrier_semaphore()

    def signal(step, carry):
        other = lax.rem(me + step, count)
        pl.semaphore_signal(
            barrier,
            inc=1,
            device_id=(other // breadth, lax.rem(other, breadth)),
            device_id_type=MESH,
        )
        return carry

    lax.fori_loop(1, count, signal, 0)
    pl.semaphore_wait(barrier, count - 1)


def gather_axis(buffer, mine, count, target, send_sems, recv_sems, skip=None):
    for step in range(1, count):
        other = lax.rem(mine + step, count)
        copy = remote(
            buffer.at[mine], buffer.at[mine], send_sems.at[step], recv_sems.at[mine], target(other)
        )
        if skip is None:
            copy.start()
        else:
            pl.when(other != skip)(copy.start)


def gather_sent(buffer, mine, count, target, send_sems, recv_sems, skip=None):
    for step in range(1, count):
        other = lax.rem(mine + step, count)
        copy = remote(
            buffer.at[mine], buffer.at[mine], send_sems.at[step], recv_sems.at[mine], target(other)
        )
        if skip is None:
            copy.wait_send()
        else:
            pl.when(other != skip)(copy.wait_send)


def gather_received(buffer, mine, count, target, send_sems, recv_sems):
    for step in range(1, count):
        other = lax.rem(mine + step, count)
        remote(
            buffer.at[other], buffer.at[other], send_sems.at[step], recv_sems.at[other], target(other)
        ).wait_recv()


def spread_kernel(
    height, breadth, own, pc, pr, stats, ex,
    local_sem, scatter_sems, role_sems, role_local, plane_sems, pc_sems, line_sems, pr_sems,
    ex_sends, ex_recvs,
):
    me_row, me_col = lax.axis_index("row"), lax.axis_index("col")
    width = own.shape[2]
    next_row = lax.rem(me_row + 1, height)
    in_plane = lambda other: (other, me_col)
    in_line = lambda other: (me_row, other)
    root = me_row == 0
    chunk = me_row * breadth + me_col
    local_role = jnp.logical_and(root, chunk // height == me_col)

    greet_all(height, breadth, me_row, me_col)

    def scatter_copy(i):
        return remote(own.at[i], pc.at[i], scatter_sems.at[i], pc_sems.at[i], (i, me_col))

    def role_copy(i):
        g = me_col * height + i
        k = lax.rem(g, breadth)
        r = g // breadth
        itself = jnp.logical_and(r == 0, k == me_col)
        return itself, remote(own.at[i], pr.at[k], role_sems.at[i], pr_sems.at[k], (r, k)), k

    def first_copy(j):
        return remote(own.at[0], pc.at[0], plane_sems.at[j], pc_sems.at[0], (j, me_col))

    @pl.when(root)
    def _():
        for i in range(1, height):
            scatter_copy(i).start()
        for i in range(height):
            itself, copy, k = role_copy(i)
            pl.when(jnp.logical_not(itself))(copy.start)
            local = pltpu.make_async_copy(own.at[i], pr.at[k], role_local)
            pl.when(itself)(local.start)
        for j in range(1, height):
            first_copy(j).start()
        whole = pltpu.make_async_copy(own, pc, local_sem)
        whole.start()
        whole.wait()

    @pl.when(local_role)
    def _():
        pltpu.make_async_copy(own.at[0], pr.at[me_col], role_local).wait()

    @pl.when(jnp.logical_not(root))
    def _():
        remote(
            pc.at[me_row], pc.at[me_row], plane_sems.at[0], pc_sems.at[me_row], (next_row, me_col)
        ).wait_recv()
        gather_axis(pc, me_row, height, in_plane, plane_sems, pc_sems, skip=0)

    @pl.when(jnp.logical_not(local_role))
    def _():
        remote(
            pr.at[me_col], pr.at[me_col], line_sems.at[0], pr_sems.at[me_col], (next_row, me_col)
        ).wait_recv()

    gather_axis(pr, me_col, breadth, in_line, line_sems, pr_sems)

    @pl.when(jnp.logical_not(root))
    def _():
        gather_received(pc, me_row, height, in_plane, plane_sems, pc_sems)

    gram = jnp.zeros((B, B), f32)
    top = jnp.zeros((B, B), f32)
    positions = lax.broadcasted_iota(jnp.int32, (width, B), 0)
    slots = lax.broadcasted_iota(jnp.int32, (width, B), 1)
    for i in range(height):
        piece = pc[i]
        start = (me_col * height + i) * width - B
        gram = gram + product_nt(piece, piece)
        onehot = jnp.where(positions + start == slots, f32(1.0), f32(0.0))
        top = top + product(piece, onehot)
    ex[me_col] = jnp.concatenate([gram, top], axis=1)
    gather_axis(ex, me_col, breadth, in_line, ex_sends, ex_recvs)
    gather_received(ex, me_col, breadth, in_line, ex_sends, ex_recvs)
    total = ex[0]
    for k in range(1, breadth):
        total = total + ex[k]
    stats[...] = total
    gather_received(pr, me_col, breadth, in_line, line_sems, pr_sems)
    gather_sent(ex, me_col, breadth, in_line, ex_sends, ex_recvs)
    gather_sent(pr, me_col, breadth, in_line, line_sems, pr_sems)

    @pl.when(root)
    def _():
        for i in range(1, height):
            scatter_copy(i).wait_send()
        for i in range(height):
            itself, copy, _ = role_copy(i)
            pl.when(jnp.logical_not(itself))(copy.wait_send)
        for j in range(1, height):
            first_copy(j).wait_send()

    @pl.when(jnp.logical_not(root))
    def _():
        gather_sent(pc, me_row, height, in_plane, plane_sems, pc_sems, skip=0)


def spread(own, height, breadth):
    width = own.shape[2]
    vmem = pl.BlockSpec(memory_space=pltpu.VMEM)
    dma = pltpu.SemaphoreType.DMA
    return pl.pallas_call(
        lambda *refs: spread_kernel(height, breadth, *refs),
        out_shape=[
            jax.ShapeDtypeStruct((height, B, width), f32),
            jax.ShapeDtypeStruct((breadth, B, width), f32),
            jax.ShapeDtypeStruct((B, 2 * B), f32),
        ],
        in_specs=[vmem],
        out_specs=[vmem] * 3,
        scratch_shapes=[
            pltpu.VMEM((breadth, B, 2 * B), f32),
            dma(()),
            dma((height,)),
            dma((height,)),
            dma(()),
            dma((height,)),
            dma((height,)),
            dma((breadth,)),
            dma((breadth,)),
            dma((breadth,)),
            dma((breadth,)),
        ],
        compiler_params=pltpu.CompilerParams(collective_id=0, has_side_effects=True),
        name="spread",
    )(own)


def vectors_kernel(height, breadth, stats, pc, pr, vc, vr, factor_ref, turned_ref):
    first, second, factor, turned = factor_values(stats[:, :B], stats[:, B:].T)
    factor_ref[...] = factor
    turned_ref[...] = turned
    width = pc.shape[2]
    slots = lax.broadcasted_iota(jnp.int32, (B, width), 0)
    positions = lax.broadcasted_iota(jnp.int32, (B, width), 1)
    for pieces, out, base, count in (
        (pc, vc, lax.axis_index("col") * height, height),
        (pr, vr, lax.axis_index("row") * breadth, breadth),
    ):
        for i in range(count):
            start = (base + i) * width - B
            onehot = jnp.where(positions + start == slots, f32(1.0), f32(0.0))
            out[:, i * width : (i + 1) * width] = product(first, pieces[i]) - product(
                second, onehot
            )


def vectors_of(stats, pc, pr, height, breadth):
    width = pc.shape[2]
    vmem = pl.BlockSpec(memory_space=pltpu.VMEM)
    return pl.pallas_call(
        lambda *refs: vectors_kernel(height, breadth, *refs),
        out_shape=[
            jax.ShapeDtypeStruct((B, height * width), f32),
            jax.ShapeDtypeStruct((B, breadth * width), f32),
            jax.ShapeDtypeStruct((B, B), f32),
            jax.ShapeDtypeStruct((B, B), f32),
        ],
        in_specs=[vmem] * 3,
        out_specs=[vmem] * 4,
        name="vectors",
    )(stats, pc, pr)


def image_kernel(
    height, breadth, z, vc, wc, wr, projected, rs, ex,
    rs_sends, rs_recvs, line_sems, wr_sems, role_sem, plane_sems, wc_sems, ex_sends, ex_recvs,
):
    me_row, me_col = lax.axis_index("row"), lax.axis_index("col")
    width = z.shape[2]
    in_plane = lambda other: (other, me_col)
    in_line = lambda other: (me_row, other)
    chunk = me_row * breadth + me_col
    to_row = lax.rem(chunk, height)
    to_col = chunk // height
    itself = jnp.logical_and(to_row == me_row, to_col == me_col)

    greet_all(height, breadth, me_row, me_col)

    def part_copy(step):
        other = lax.rem(me_col + step, breadth)
        return remote(
            z.at[other], rs.at[me_col], rs_sends.at[step], rs_recvs.at[me_col], in_line(other)
        )

    for step in range(1, breadth):
        part_copy(step).start()
    rs[me_col] = z[me_col]
    gather_received(rs, me_col, breadth, in_line, rs_sends, rs_recvs)
    total = rs[0]
    for k in range(1, breadth):
        total = total + rs[k]
    wr[me_col] = total
    role = remote(wr.at[me_col], wc.at[to_row], role_sem, wc_sems.at[to_row], (to_row, to_col))

    @pl.when(jnp.logical_not(itself))
    def _():
        role.start()

    gather_axis(wr, me_col, breadth, in_line, line_sems, wr_sems)

    @pl.when(itself)
    def _():
        wc[me_row] = total

    @pl.when(jnp.logical_not(itself))
    def _():
        remote(
            wc.at[me_row], wc.at[me_row], plane_sems.at[0], wc_sems.at[me_row],
            (lax.rem(me_row + 1, height), me_col),
        ).wait_recv()

    gather_axis(wc, me_row, height, in_plane, plane_sems, wc_sems)
    gather_received(wc, me_row, height, in_plane, plane_sems, wc_sems)
    partial = jnp.zeros((B, B), f32)
    for i in range(height):
        partial = partial + product_nt(wc[i], vc[:, i * width : (i + 1) * width])
    ex[me_col] = jnp.concatenate([partial, jnp.zeros((B, B), f32)], axis=1)
    gather_axis(ex, me_col, breadth, in_line, ex_sends, ex_recvs)
    gather_received(ex, me_col, breadth, in_line, ex_sends, ex_recvs)
    summed = ex[0]
    for k in range(1, breadth):
        summed = summed + ex[k]
    projected[...] = summed
    gather_received(wr, me_col, breadth, in_line, line_sems, wr_sems)
    for step in range(1, breadth):
        part_copy(step).wait_send()

    @pl.when(jnp.logical_not(itself))
    def _():
        role.wait_send()

    gather_sent(wr, me_col, breadth, in_line, line_sems, wr_sems)
    gather_sent(wc, me_row, height, in_plane, plane_sems, wc_sems)
    gather_sent(ex, me_col, breadth, in_line, ex_sends, ex_recvs)


def images(z, vc, height, breadth):
    width = z.shape[2]
    vmem = pl.BlockSpec(memory_space=pltpu.VMEM)
    dma = pltpu.SemaphoreType.DMA
    return pl.pallas_call(
        lambda *refs: image_kernel(height, breadth, *refs),
        out_shape=[
            jax.ShapeDtypeStruct((height, B, width), f32),
            jax.ShapeDtypeStruct((breadth, B, width), f32),
            jax.ShapeDtypeStruct((B, 2 * B), f32),
        ],
        in_specs=[vmem] * 2,
        out_specs=[vmem] * 3,
        scratch_shapes=[
            pltpu.VMEM((breadth, B, width), f32),
            pltpu.VMEM((breadth, B, 2 * B), f32),
            dma((breadth,)),
            dma((breadth,)),
            dma((breadth,)),
            dma((breadth,)),
            dma(()),
            dma((height,)),
            dma((height,)),
            dma((breadth,)),
            dma((breadth,)),
        ],
        compiler_params=pltpu.CompilerParams(collective_id=1, has_side_effects=True),
        name="images",
    )(z, vc)


def updates_kernel(height, breadth, projected, factor, turned, vc, vr, wc, wr, left, right):
    inner = product(turned[...], product(projected[:, :B], factor[...]))
    width = wc.shape[2]
    right[B:, :] = vc[...]
    left[:B, :] = vr[...]
    for i in range(height):
        part = slice(i * width, (i + 1) * width)
        right[:B, part] = product(turned[...], wc[i]) - 0.5 * product(inner, vc[:, part])
    for i in range(breadth):
        part = slice(i * width, (i + 1) * width)
        left[B:, part] = product(turned[...], wr[i]) - 0.5 * product(inner, vr[:, part])


def updates(projected, factor, turned, vc, vr, wc, wr):
    height, breadth = wc.shape[0], wr.shape[0]
    vmem = pl.BlockSpec(memory_space=pltpu.VMEM)
    return pl.pallas_call(
        lambda *refs: updates_kernel(height, breadth, *refs),
        out_shape=[
            jax.ShapeDtypeStruct((2 * B, vr.shape[1]), f32),
            jax.ShapeDtypeStruct((2 * B, vc.shape[1]), f32),
        ],
        in_specs=[vmem] * 7,
        out_specs=[vmem] * 2,
        name="updates",
    )(projected, factor, turned, vc, vr, wc, wr)


def shards(height, breadth, matrix):
    rows, cols = matrix.shape
    width = cols // height
    global_cols = lax.axis_index("col") * cols + jnp.arange(cols, dtype=jnp.int32)
    masked = jnp.where(global_cols[None, :] >= B, matrix[0:B, :], f32(0.0))
    own = masked.reshape(B, height, width).transpose(1, 0, 2)
    pc, pr, stats = spread(own, height, breadth)
    vc, vr, factor, turned = vectors_of(stats, pc, pr, height, breadth)
    image = lax.dot_general(
        vc, matrix, (((1,), (1,)), ((), ())), precision=high, preferred_element_type=f32
    )
    z = image.reshape(B, breadth, width).transpose(1, 0, 2)
    wc, wr, projected = images(z, vc, height, breadth)
    left, right = updates(projected, factor, turned, vc, vr, wc, wr)
    return matrix - lax.dot_general(
        left, right, (((0,), (0,)), ((), ())), precision=high, preferred_element_type=f32
    )


def solution(mesh):
    placed = (P("row", "col"),)
    height, breadth = mesh.shape["row"], mesh.shape["col"]
    return jax.shard_map(
        lambda matrix: shards(height, breadth, matrix),
        mesh=mesh,
        in_specs=placed,
        out_specs=P("row", "col"),
        check_vma=False,
    )
```

```python
import jax
import jax.numpy as jnp
from jax import lax
from jax.experimental import pallas as pl
from jax.experimental.pallas import tpu as pltpu
from jax.sharding import PartitionSpec as P

B = 64


highest = lax.Precision.HIGHEST
MESH = pl.DeviceIdType.MESH
f32 = jnp.float32
bf16 = jnp.bfloat16


def product(left, right):
    return jnp.dot(left, right, precision=highest, preferred_element_type=f32)


def split(x):
    upper = x.astype(bf16)
    return upper, (x - upper.astype(f32)).astype(bf16)


def product_nt(left, right):
    return lax.dot_general(
        left, right, (((1,), (1,)), ((), ())), precision=highest, preferred_element_type=f32
    )


def factor_values(gram, top):
    rows = lax.broadcasted_iota(jnp.int32, (B, 2 * B), 0)
    lanes = lax.broadcasted_iota(jnp.int32, (B, 2 * B), 1)
    eye = jnp.where(rows + B == lanes, f32(1.0), f32(0.0))
    small_rows = lax.broadcasted_iota(jnp.int32, (B, B), 0)
    small_lanes = lax.broadcasted_iota(jnp.int32, (B, B), 1)
    eye_half = jnp.where(small_rows == small_lanes, f32(1.0), f32(0.0))
    work = jnp.concatenate([gram, eye_half], axis=1)
    for j in range(B):
        inverse = 1.0 / jnp.sqrt(work[j : j + 1, j : j + 1])
        row = work[j : j + 1, :] * inverse
        column = work[:, j : j + 1] * inverse
        lowered = work - column * row
        work = jnp.where(rows > j, lowered, jnp.where(rows == j, row, work))
    lower_inverse = work[:, B:]
    top_basis = product_nt(top, lower_inverse)
    top_turned = product_nt(lower_inverse, top)
    q = jnp.concatenate([top_basis, eye_half], axis=1)
    t = jnp.concatenate([top_turned, eye_half], axis=1)
    signs = jnp.zeros((1, B), f32)
    sign_lane = lax.broadcasted_iota(jnp.int32, (1, B), 1)
    reciprocals = jnp.zeros((B, 1), f32)
    sublane = lax.broadcasted_iota(jnp.int32, (B, 1), 0)
    one_row = lax.broadcasted_iota(jnp.int32, (1, 2 * B), 1)
    for j in range(B):
        pivot = q[j : j + 1, j : j + 1]
        sign = jnp.where(pivot >= 0, f32(-1.0), f32(1.0))
        inverse = 1.0 / (pivot - sign)
        row_q = q[j : j + 1, :] - jnp.where(one_row == j, sign, f32(0.0))
        row_t = t[j : j + 1, :] - jnp.where(one_row == j, sign, f32(0.0))
        below_q = q[:, j : j + 1] * inverse
        below_t = t[:, j : j + 1] * inverse
        q = jnp.where(rows > j, q - below_q * row_q, jnp.where(rows == j, row_q, q))
        t = jnp.where(rows > j, t - below_t * row_t, t)
        signs = jnp.where(sign_lane == j, sign, signs)
        reciprocals = jnp.where(sublane == j, inverse, reciprocals)
    upper = jnp.where(small_lanes >= small_rows, q[:, :B], f32(0.0))
    unit_inverse = q[:, B:]
    upper_inverse_turned = t[:, B:] * reciprocals
    factor = -product_nt(upper * signs, unit_inverse)
    factor_turned = -product_nt(unit_inverse, upper * signs)
    first = product(upper_inverse_turned, lower_inverse)
    second = upper_inverse_turned * signs
    return first, second, factor, factor_turned


def remote(src, dst, send_sem, recv_sem, device):
    return pltpu.make_async_remote_copy(
        src_ref=src,
        dst_ref=dst,
        send_sem=send_sem,
        recv_sem=recv_sem,
        device_id=device,
        device_id_type=MESH,
    )


def greet_all(height, breadth, me_row, me_col):
    count = height * breadth
    me = me_row * breadth + me_col
    barrier = pltpu.get_barrier_semaphore()

    def signal(step, carry):
        other = lax.rem(me + step, count)
        pl.semaphore_signal(
            barrier,
            inc=1,
            device_id=(other // breadth, lax.rem(other, breadth)),
            device_id_type=MESH,
        )
        return carry

    lax.fori_loop(1, count, signal, 0)
    pl.semaphore_wait(barrier, count - 1)


def gather_axis(buffer, mine, count, target, send_sems, recv_sems, skip=None):
    for step in range(1, count):
        other = lax.rem(mine + step, count)
        copy = remote(
            buffer.at[mine], buffer.at[mine], send_sems.at[step], recv_sems.at[mine], target(other)
        )
        if skip is None:
            copy.start()
        else:
            pl.when(other != skip)(copy.start)


def gather_sent(buffer, mine, count, target, send_sems, recv_sems, skip=None):
    for step in range(1, count):
        other = lax.rem(mine + step, count)
        copy = remote(
            buffer.at[mine], buffer.at[mine], send_sems.at[step], recv_sems.at[mine], target(other)
        )
        if skip is None:
            copy.wait_send()
        else:
            pl.when(other != skip)(copy.wait_send)


def gather_received(buffer, mine, count, target, send_sems, recv_sems):
    for step in range(1, count):
        other = lax.rem(mine + step, count)
        remote(
            buffer.at[other], buffer.at[other], send_sems.at[step], recv_sems.at[other], target(other)
        ).wait_recv()


def spread_kernel(
    height, breadth, own, pc, pr, stats, ex,
    local_sem, scatter_sems, role_sems, role_local, plane_sems, pc_sems, line_sems, pr_sems,
    ex_sends, ex_recvs,
):
    me_row, me_col = lax.axis_index("row"), lax.axis_index("col")
    width = own.shape[2]
    next_row = lax.rem(me_row + 1, height)
    in_plane = lambda other: (other, me_col)
    in_line = lambda other: (me_row, other)
    root = me_row == 0
    chunk = me_row * breadth + me_col
    local_role = jnp.logical_and(root, chunk // height == me_col)

    greet_all(height, breadth, me_row, me_col)

    def scatter_copy(i):
        return remote(own.at[i], pc.at[i], scatter_sems.at[i], pc_sems.at[i], (i, me_col))

    def role_copy(i):
        g = me_col * height + i
        k = lax.rem(g, breadth)
        r = g // breadth
        itself = jnp.logical_and(r == 0, k == me_col)
        return itself, remote(own.at[i], pr.at[k], role_sems.at[i], pr_sems.at[k], (r, k)), k

    def first_copy(j):
        return remote(own.at[0], pc.at[0], plane_sems.at[j], pc_sems.at[0], (j, me_col))

    @pl.when(root)
    def _():
        for i in range(1, height):
            scatter_copy(i).start()
        for i in range(height):
            itself, copy, k = role_copy(i)
            pl.when(jnp.logical_not(itself))(copy.start)
            local = pltpu.make_async_copy(own.at[i], pr.at[k], role_local)
            pl.when(itself)(local.start)
        for j in range(1, height):
            first_copy(j).start()
        whole = pltpu.make_async_copy(own, pc, local_sem)
        whole.start()
        whole.wait()

    @pl.when(local_role)
    def _():
        pltpu.make_async_copy(own.at[0], pr.at[me_col], role_local).wait()

    @pl.when(jnp.logical_not(root))
    def _():
        remote(
            pc.at[me_row], pc.at[me_row], plane_sems.at[0], pc_sems.at[me_row], (next_row, me_col)
        ).wait_recv()
        gather_axis(pc, me_row, height, in_plane, plane_sems, pc_sems, skip=0)

    @pl.when(jnp.logical_not(local_role))
    def _():
        remote(
            pr.at[me_col], pr.at[me_col], line_sems.at[0], pr_sems.at[me_col], (next_row, me_col)
        ).wait_recv()

    gather_axis(pr, me_col, breadth, in_line, line_sems, pr_sems)

    @pl.when(jnp.logical_not(root))
    def _():
        gather_received(pc, me_row, height, in_plane, plane_sems, pc_sems)

    gram = jnp.zeros((B, B), f32)
    top = jnp.zeros((B, B), f32)
    positions = lax.broadcasted_iota(jnp.int32, (width, B), 0)
    slots = lax.broadcasted_iota(jnp.int32, (width, B), 1)
    for i in range(height):
        piece = pc[i]
        start = (me_col * height + i) * width - B
        gram = gram + product_nt(piece, piece)
        onehot = jnp.where(positions + start == slots, f32(1.0), f32(0.0))
        top = top + product(piece, onehot)
    ex[me_col] = jnp.concatenate([gram, top], axis=1)
    gather_axis(ex, me_col, breadth, in_line, ex_sends, ex_recvs)
    gather_received(ex, me_col, breadth, in_line, ex_sends, ex_recvs)
    total = ex[0]
    for k in range(1, breadth):
        total = total + ex[k]
    stats[...] = total
    gather_received(pr, me_col, breadth, in_line, line_sems, pr_sems)
    gather_sent(ex, me_col, breadth, in_line, ex_sends, ex_recvs)
    gather_sent(pr, me_col, breadth, in_line, line_sems, pr_sems)

    @pl.when(root)
    def _():
        for i in range(1, height):
            scatter_copy(i).wait_send()
        for i in range(height):
            itself, copy, _ = role_copy(i)
            pl.when(jnp.logical_not(itself))(copy.wait_send)
        for j in range(1, height):
            first_copy(j).wait_send()

    @pl.when(jnp.logical_not(root))
    def _():
        gather_sent(pc, me_row, height, in_plane, plane_sems, pc_sems, skip=0)


def spread(own, height, breadth):
    width = own.shape[2]
    vmem = pl.BlockSpec(memory_space=pltpu.VMEM)
    dma = pltpu.SemaphoreType.DMA
    return pl.pallas_call(
        lambda *refs: spread_kernel(height, breadth, *refs),
        out_shape=[
            jax.ShapeDtypeStruct((height, B, width), f32),
            jax.ShapeDtypeStruct((breadth, B, width), f32),
            jax.ShapeDtypeStruct((B, 2 * B), f32),
        ],
        in_specs=[vmem],
        out_specs=[vmem] * 3,
        scratch_shapes=[
            pltpu.VMEM((breadth, B, 2 * B), f32),
            dma(()),
            dma((height,)),
            dma((height,)),
            dma(()),
            dma((height,)),
            dma((height,)),
            dma((breadth,)),
            dma((breadth,)),
            dma((breadth,)),
            dma((breadth,)),
        ],
        compiler_params=pltpu.CompilerParams(collective_id=0, has_side_effects=True),
        name="spread",
    )(own)


def vectors_kernel(height, breadth, stats, pc, pr, vc, vr, factor_ref, turned_ref, halves):
    first, second, factor, turned = factor_values(stats[:, :B], stats[:, B:].T)
    factor_ref[...] = factor
    turned_ref[...] = turned
    width = pc.shape[2]
    slots = lax.broadcasted_iota(jnp.int32, (B, width), 0)
    positions = lax.broadcasted_iota(jnp.int32, (B, width), 1)
    for pieces, out, base, count in (
        (pc, vc, lax.axis_index("col") * height, height),
        (pr, vr, lax.axis_index("row") * breadth, breadth),
    ):
        for i in range(count):
            start = (base + i) * width - B
            onehot = jnp.where(positions + start == slots, f32(1.0), f32(0.0))
            out[:, i * width : (i + 1) * width] = product(first, pieces[i]) - product(
                second, onehot
            )
    upper, lower = split(vc[...])
    halves[:B, :] = upper
    halves[B:, :] = lower


def vectors_of(stats, pc, pr, height, breadth):
    width = pc.shape[2]
    vmem = pl.BlockSpec(memory_space=pltpu.VMEM)
    return pl.pallas_call(
        lambda *refs: vectors_kernel(height, breadth, *refs),
        out_shape=[
            jax.ShapeDtypeStruct((B, height * width), f32),
            jax.ShapeDtypeStruct((B, breadth * width), f32),
            jax.ShapeDtypeStruct((B, B), f32),
            jax.ShapeDtypeStruct((B, B), f32),
            jax.ShapeDtypeStruct((2 * B, height * width), bf16),
        ],
        in_specs=[vmem] * 3,
        out_specs=[vmem] * 5,
        name="vectors",
    )(stats, pc, pr)


def image_kernel(
    height, breadth, z, vc, wc, wr, projected, rs, ex,
    rs_sends, rs_recvs, line_sems, wr_sems, role_sem, plane_sems, wc_sems, ex_sends, ex_recvs,
):
    me_row, me_col = lax.axis_index("row"), lax.axis_index("col")
    width = z.shape[2]
    in_plane = lambda other: (other, me_col)
    in_line = lambda other: (me_row, other)
    chunk = me_row * breadth + me_col
    to_row = lax.rem(chunk, height)
    to_col = chunk // height
    itself = jnp.logical_and(to_row == me_row, to_col == me_col)

    greet_all(height, breadth, me_row, me_col)

    def part_copy(step):
        other = lax.rem(me_col + step, breadth)
        return remote(
            z.at[other], rs.at[me_col], rs_sends.at[step], rs_recvs.at[me_col], in_line(other)
        )

    for step in range(1, breadth):
        part_copy(step).start()
    rs[me_col] = z[me_col]
    gather_received(rs, me_col, breadth, in_line, rs_sends, rs_recvs)
    total = rs[0]
    for k in range(1, breadth):
        total = total + rs[k]
    wr[me_col] = total
    role = remote(wr.at[me_col], wc.at[to_row], role_sem, wc_sems.at[to_row], (to_row, to_col))

    @pl.when(jnp.logical_not(itself))
    def _():
        role.start()

    gather_axis(wr, me_col, breadth, in_line, line_sems, wr_sems)

    @pl.when(itself)
    def _():
        wc[me_row] = total

    @pl.when(jnp.logical_not(itself))
    def _():
        remote(
            wc.at[me_row], wc.at[me_row], plane_sems.at[0], wc_sems.at[me_row],
            (lax.rem(me_row + 1, height), me_col),
        ).wait_recv()

    gather_axis(wc, me_row, height, in_plane, plane_sems, wc_sems)
    gather_received(wc, me_row, height, in_plane, plane_sems, wc_sems)
    partial = jnp.zeros((B, B), f32)
    for i in range(height):
        partial = partial + product_nt(wc[i], vc[:, i * width : (i + 1) * width])
    ex[me_col] = jnp.concatenate([partial, jnp.zeros((B, B), f32)], axis=1)
    gather_axis(ex, me_col, breadth, in_line, ex_sends, ex_recvs)
    gather_received(ex, me_col, breadth, in_line, ex_sends, ex_recvs)
    summed = ex[0]
    for k in range(1, breadth):
        summed = summed + ex[k]
    projected[...] = summed
    gather_received(wr, me_col, breadth, in_line, line_sems, wr_sems)
    for step in range(1, breadth):
        part_copy(step).wait_send()

    @pl.when(jnp.logical_not(itself))
    def _():
        role.wait_send()

    gather_sent(wr, me_col, breadth, in_line, line_sems, wr_sems)
    gather_sent(wc, me_row, height, in_plane, plane_sems, wc_sems)
    gather_sent(ex, me_col, breadth, in_line, ex_sends, ex_recvs)


def images(z, vc, height, breadth):
    width = z.shape[2]
    vmem = pl.BlockSpec(memory_space=pltpu.VMEM)
    dma = pltpu.SemaphoreType.DMA
    return pl.pallas_call(
        lambda *refs: image_kernel(height, breadth, *refs),
        out_shape=[
            jax.ShapeDtypeStruct((height, B, width), f32),
            jax.ShapeDtypeStruct((breadth, B, width), f32),
            jax.ShapeDtypeStruct((B, 2 * B), f32),
        ],
        in_specs=[vmem] * 2,
        out_specs=[vmem] * 3,
        scratch_shapes=[
            pltpu.VMEM((breadth, B, width), f32),
            pltpu.VMEM((breadth, B, 2 * B), f32),
            dma((breadth,)),
            dma((breadth,)),
            dma((breadth,)),
            dma((breadth,)),
            dma(()),
            dma((height,)),
            dma((height,)),
            dma((breadth,)),
            dma((breadth,)),
        ],
        compiler_params=pltpu.CompilerParams(collective_id=1, has_side_effects=True),
        name="images",
    )(z, vc)


def image_part_kernel(block, halves, out):
    nt = (((1,), (1,)), ((), ()))
    rows, cols = block.shape
    size = min(512, cols)
    both = jnp.zeros((rows, 2 * B), f32)
    for start in range(0, cols, size):
        part = slice(start, start + size)
        upper, lower = split(block[:, part])
        both = both + lax.dot_general(upper, halves[:, part], nt, preferred_element_type=f32)
        low = lax.dot_general(lower, halves[:, part], nt, preferred_element_type=f32)
        both = both + jnp.where(lax.broadcasted_iota(jnp.int32, both.shape, 1) < B, low, f32(0.0))
    turned = both.T
    out[0] = turned[:B, :] + turned[B:, :]


def image_part(matrix, halves, width):
    rows, cols = matrix.shape
    return pl.pallas_call(
        image_part_kernel,
        grid=(rows // width,),
        out_shape=jax.ShapeDtypeStruct((rows // width, B, width), f32),
        in_specs=[
            pl.BlockSpec((width, cols), lambda i: (i, 0)),
            pl.BlockSpec((2 * B, cols), lambda i: (0, 0)),
        ],
        out_specs=pl.BlockSpec((1, B, width), lambda i: (i, 0, 0)),
        name="image_part",
    )(matrix, halves)


def final_kernel(block, left, right, out):
    cols = block.shape[1]
    size = min(512, cols)
    for start in range(0, cols, size):
        part = slice(start, start + size)
        out[:, part] = block[:, part] - jnp.dot(
            left[...], right[:, part], preferred_element_type=f32
        )


def final(matrix, left, right):
    rows, cols = matrix.shape
    tile = min(256, rows)
    depth = left.shape[1]
    return pl.pallas_call(
        final_kernel,
        grid=(rows // tile,),
        out_shape=jax.ShapeDtypeStruct((rows, cols), f32),
        in_specs=[
            pl.BlockSpec((tile, cols), lambda i: (i, 0)),
            pl.BlockSpec((tile, depth), lambda i: (i, 0)),
            pl.BlockSpec((depth, cols), lambda i: (0, 0)),
        ],
        out_specs=pl.BlockSpec((tile, cols), lambda i: (i, 0)),
        name="final",
    )(matrix, left, right)


def updates_kernel(height, breadth, projected, factor, turned, vc, vr, wc, wr, left, right):
    inner = product(turned[...], product(projected[:, :B], factor[...]))
    mix = jnp.concatenate([turned[...], -0.5 * inner], axis=1)
    width = wc.shape[2]
    for i in range(height):
        part = slice(i * width, (i + 1) * width)
        v = vc[:, part]
        u = product(mix, jnp.concatenate([wc[i], v], axis=0))
        upper, lower = split(jnp.concatenate([u, v], axis=0))
        right[: 2 * B, part] = upper
        right[2 * B : 4 * B, part] = upper
        right[4 * B :, part] = lower
    for i in range(breadth):
        part = slice(i * width, (i + 1) * width)
        v = vr[:, part]
        u = product(mix, jnp.concatenate([wr[i], v], axis=0))
        upper, lower = split(jnp.concatenate([v, u], axis=0).T)
        left[part, : 2 * B] = upper
        left[part, 2 * B : 4 * B] = lower
        left[part, 4 * B :] = upper


def updates(projected, factor, turned, vc, vr, wc, wr):
    height, breadth = wc.shape[0], wr.shape[0]
    vmem = pl.BlockSpec(memory_space=pltpu.VMEM)
    return pl.pallas_call(
        lambda *refs: updates_kernel(height, breadth, *refs),
        out_shape=[
            jax.ShapeDtypeStruct((vr.shape[1], 6 * B), bf16),
            jax.ShapeDtypeStruct((6 * B, vc.shape[1]), bf16),
        ],
        in_specs=[vmem] * 7,
        out_specs=[vmem] * 2,
        name="updates",
    )(projected, factor, turned, vc, vr, wc, wr)


def shards(height, breadth, matrix):
    rows, cols = matrix.shape
    width = cols // height
    global_cols = lax.axis_index("col") * cols + jnp.arange(cols, dtype=jnp.int32)
    masked = jnp.where(global_cols[None, :] >= B, matrix[0:B, :], f32(0.0))
    own = masked.reshape(B, height, width).transpose(1, 0, 2)
    pc, pr, stats = spread(own, height, breadth)
    vc, vr, factor, turned, halves = vectors_of(stats, pc, pr, height, breadth)
    z = image_part(matrix, halves, width)
    wc, wr, projected = images(z, vc, height, breadth)
    left, right = updates(projected, factor, turned, vc, vr, wc, wr)
    return final(matrix, left, right)


def solution(mesh):
    placed = (P("row", "col"),)
    height, breadth = mesh.shape["row"], mesh.shape["col"]
    return jax.shard_map(
        lambda matrix: shards(height, breadth, matrix),
        mesh=mesh,
        in_specs=placed,
        out_specs=P("row", "col"),
        check_vma=False,
    )
```

```python
import jax
import jax.numpy as jnp
from jax import lax
from jax.experimental import pallas as pl
from jax.experimental.pallas import tpu as pltpu
from jax.sharding import PartitionSpec as P

B = 64


highest = lax.Precision.HIGHEST
MESH = pl.DeviceIdType.MESH
f32 = jnp.float32
bf16 = jnp.bfloat16


def product(left, right):
    return jnp.dot(left, right, precision=highest, preferred_element_type=f32)


def split(x):
    upper = x.astype(bf16)
    return upper, (x - upper.astype(f32)).astype(bf16)


def product_nt(left, right):
    return lax.dot_general(
        left, right, (((1,), (1,)), ((), ())), precision=highest, preferred_element_type=f32
    )


def factor_values(gram, top):
    rows = lax.broadcasted_iota(jnp.int32, (B, 2 * B), 0)
    lanes = lax.broadcasted_iota(jnp.int32, (B, 2 * B), 1)
    eye = jnp.where(rows + B == lanes, f32(1.0), f32(0.0))
    small_rows = lax.broadcasted_iota(jnp.int32, (B, B), 0)
    small_lanes = lax.broadcasted_iota(jnp.int32, (B, B), 1)
    eye_half = jnp.where(small_rows == small_lanes, f32(1.0), f32(0.0))
    work = jnp.concatenate([gram, eye_half], axis=1)
    for j in range(B):
        inverse = 1.0 / jnp.sqrt(work[j : j + 1, j : j + 1])
        row = work[j : j + 1, :] * inverse
        column = work[:, j : j + 1] * inverse
        lowered = work - column * row
        work = jnp.where(rows > j, lowered, jnp.where(rows == j, row, work))
    lower_inverse = work[:, B:]
    top_basis = product_nt(top, lower_inverse)
    top_turned = product_nt(lower_inverse, top)
    q = jnp.concatenate([top_basis, eye_half], axis=1)
    t = jnp.concatenate([top_turned, eye_half], axis=1)
    signs = jnp.zeros((1, B), f32)
    sign_lane = lax.broadcasted_iota(jnp.int32, (1, B), 1)
    reciprocals = jnp.zeros((B, 1), f32)
    sublane = lax.broadcasted_iota(jnp.int32, (B, 1), 0)
    one_row = lax.broadcasted_iota(jnp.int32, (1, 2 * B), 1)
    for j in range(B):
        pivot = q[j : j + 1, j : j + 1]
        sign = jnp.where(pivot >= 0, f32(-1.0), f32(1.0))
        inverse = 1.0 / (pivot - sign)
        row_q = q[j : j + 1, :] - jnp.where(one_row == j, sign, f32(0.0))
        row_t = t[j : j + 1, :] - jnp.where(one_row == j, sign, f32(0.0))
        below_q = q[:, j : j + 1] * inverse
        below_t = t[:, j : j + 1] * inverse
        q = jnp.where(rows > j, q - below_q * row_q, jnp.where(rows == j, row_q, q))
        t = jnp.where(rows > j, t - below_t * row_t, t)
        signs = jnp.where(sign_lane == j, sign, signs)
        reciprocals = jnp.where(sublane == j, inverse, reciprocals)
    upper = jnp.where(small_lanes >= small_rows, q[:, :B], f32(0.0))
    unit_inverse = q[:, B:]
    upper_inverse_turned = t[:, B:] * reciprocals
    factor = -product_nt(upper * signs, unit_inverse)
    factor_turned = -product_nt(unit_inverse, upper * signs)
    first = product(upper_inverse_turned, lower_inverse)
    second = upper_inverse_turned * signs
    return first, second, factor, factor_turned


def remote(src, dst, send_sem, recv_sem, device):
    return pltpu.make_async_remote_copy(
        src_ref=src,
        dst_ref=dst,
        send_sem=send_sem,
        recv_sem=recv_sem,
        device_id=device,
        device_id_type=MESH,
    )


def greet_all(height, breadth, me_row, me_col):
    count = height * breadth
    me = me_row * breadth + me_col
    barrier = pltpu.get_barrier_semaphore()

    def signal(step, carry):
        other = lax.rem(me + step, count)
        pl.semaphore_signal(
            barrier,
            inc=1,
            device_id=(other // breadth, lax.rem(other, breadth)),
            device_id_type=MESH,
        )
        return carry

    lax.fori_loop(1, count, signal, 0)
    pl.semaphore_wait(barrier, count - 1)


def gather_axis(buffer, mine, count, target, send_sems, recv_sems, skip=None):
    for step in range(1, count):
        other = lax.rem(mine + step, count)
        copy = remote(
            buffer.at[mine], buffer.at[mine], send_sems.at[step], recv_sems.at[mine], target(other)
        )
        if skip is None:
            copy.start()
        else:
            pl.when(other != skip)(copy.start)


def gather_sent(buffer, mine, count, target, send_sems, recv_sems, skip=None):
    for step in range(1, count):
        other = lax.rem(mine + step, count)
        copy = remote(
            buffer.at[mine], buffer.at[mine], send_sems.at[step], recv_sems.at[mine], target(other)
        )
        if skip is None:
            copy.wait_send()
        else:
            pl.when(other != skip)(copy.wait_send)


def gather_received(buffer, mine, count, target, send_sems, recv_sems):
    for step in range(1, count):
        other = lax.rem(mine + step, count)
        remote(
            buffer.at[other], buffer.at[other], send_sems.at[step], recv_sems.at[other], target(other)
        ).wait_recv()


def pair_copies(buffer, mine, count, target, send_sems, recv_sems, skip):
    partner = mine + 1 - 2 * lax.rem(mine, 2)

    def copy(slot, step, other):
        made = remote(
            buffer.at[slot], buffer.at[slot], send_sems.at[step], recv_sems.at[slot], target(other)
        )
        return other != skip, made

    direct = []
    passed = []
    for step in range(2, count, 2):
        other = lax.rem(mine + step, count)
        direct.append(copy(mine, step, other))
        passed.append((other, copy(other, step + 1, partner)))
    direct.append(copy(mine, 1, partner))
    return partner, direct, passed


def pair_gather(buffer, mine, count, target, send_sems, recv_sems, skip=-1):
    partner, direct, passed = pair_copies(buffer, mine, count, target, send_sems, recv_sems, skip)

    def received(slot):
        remote(
            buffer.at[slot], buffer.at[slot], send_sems.at[0], recv_sems.at[slot], target(partner)
        ).wait_recv()

    for allowed, copy in direct:
        pl.when(allowed)(copy.start)
    for slot, (allowed, copy) in passed:
        received(slot)
        pl.when(allowed)(copy.start)
    received(partner)
    for step in range(2, count, 2):
        received(lax.rem(partner + step, count))


def pair_sent(buffer, mine, count, target, send_sems, recv_sems, skip=-1):
    _, direct, passed = pair_copies(buffer, mine, count, target, send_sems, recv_sems, skip)
    for allowed, copy in direct + [entry for _, entry in passed]:
        pl.when(allowed)(copy.wait_send)


def spread_kernel(
    height, breadth, own, pc, pr, stats, ex,
    local_sem, scatter_sems, role_sems, role_local, plane_sems, pc_sems, line_sems, pr_sems,
    ex_sends, ex_recvs,
):
    me_row, me_col = lax.axis_index("row"), lax.axis_index("col")
    width = own.shape[2]
    next_row = lax.rem(me_row + 1, height)
    in_plane = lambda other: (other, me_col)
    in_line = lambda other: (me_row, other)
    root = me_row == 0
    chunk = me_row * breadth + me_col
    local_role = jnp.logical_and(root, chunk // height == me_col)

    greet_all(height, breadth, me_row, me_col)

    def scatter_copy(i):
        return remote(own.at[i], pc.at[i], scatter_sems.at[i], pc_sems.at[i], (i, me_col))

    def role_copy(i):
        g = me_col * height + i
        k = lax.rem(g, breadth)
        r = g // breadth
        itself = jnp.logical_and(r == 0, k == me_col)
        return itself, remote(own.at[i], pr.at[k], role_sems.at[i], pr_sems.at[k], (r, k)), k

    def first_copies():
        made = [
            remote(own.at[0], pc.at[0], plane_sems.at[j], pc_sems.at[0], (j, me_col))
            for j in [1] + list(range(2, height, 2))
        ]
        return made + [
            remote(own.at[m], pc.at[m], plane_sems.at[m + 1], pc_sems.at[m], (1, me_col))
            for m in range(2, height, 2)
        ]

    @pl.when(root)
    def _():
        for i in range(1, height):
            scatter_copy(i).start()
        for i in range(height):
            itself, copy, k = role_copy(i)
            pl.when(jnp.logical_not(itself))(copy.start)
            local = pltpu.make_async_copy(own.at[i], pr.at[k], role_local)
            pl.when(itself)(local.start)
        for copy in first_copies():
            copy.start()
        whole = pltpu.make_async_copy(own, pc, local_sem)
        whole.start()
        whole.wait()

    @pl.when(local_role)
    def _():
        pltpu.make_async_copy(own.at[0], pr.at[me_col], role_local).wait()

    @pl.when(jnp.logical_not(root))
    def _():
        remote(
            pc.at[me_row], pc.at[me_row], plane_sems.at[0], pc_sems.at[me_row], (next_row, me_col)
        ).wait_recv()

    @pl.when(jnp.logical_not(local_role))
    def _():
        remote(
            pr.at[me_col], pr.at[me_col], line_sems.at[0], pr_sems.at[me_col], (next_row, me_col)
        ).wait_recv()

    gather_axis(pr, me_col, breadth, in_line, line_sems, pr_sems)

    @pl.when(jnp.logical_not(root))
    def _():
        pair_gather(pc, me_row, height, in_plane, plane_sems, pc_sems, skip=0)

    gram = jnp.zeros((B, B), f32)
    top = jnp.zeros((B, B), f32)
    positions = lax.broadcasted_iota(jnp.int32, (width, B), 0)
    slots = lax.broadcasted_iota(jnp.int32, (width, B), 1)
    for i in range(height):
        piece = pc[i]
        start = (me_col * height + i) * width - B
        gram = gram + product_nt(piece, piece)
        onehot = jnp.where(positions + start == slots, f32(1.0), f32(0.0))
        top = top + product(piece, onehot)
    ex[me_col] = jnp.concatenate([gram, top], axis=1)
    gather_axis(ex, me_col, breadth, in_line, ex_sends, ex_recvs)
    gather_received(ex, me_col, breadth, in_line, ex_sends, ex_recvs)
    total = ex[0]
    for k in range(1, breadth):
        total = total + ex[k]
    stats[...] = total
    gather_received(pr, me_col, breadth, in_line, line_sems, pr_sems)
    gather_sent(ex, me_col, breadth, in_line, ex_sends, ex_recvs)
    gather_sent(pr, me_col, breadth, in_line, line_sems, pr_sems)

    @pl.when(root)
    def _():
        for i in range(1, height):
            scatter_copy(i).wait_send()
        for i in range(height):
            itself, copy, _ = role_copy(i)
            pl.when(jnp.logical_not(itself))(copy.wait_send)
        for copy in first_copies():
            copy.wait_send()

    @pl.when(jnp.logical_not(root))
    def _():
        pair_sent(pc, me_row, height, in_plane, plane_sems, pc_sems, skip=0)


def spread(own, height, breadth):
    width = own.shape[2]
    vmem = pl.BlockSpec(memory_space=pltpu.VMEM)
    dma = pltpu.SemaphoreType.DMA
    return pl.pallas_call(
        lambda *refs: spread_kernel(height, breadth, *refs),
        out_shape=[
            jax.ShapeDtypeStruct((height, B, width), f32),
            jax.ShapeDtypeStruct((breadth, B, width), f32),
            jax.ShapeDtypeStruct((B, 2 * B), f32),
        ],
        in_specs=[vmem],
        out_specs=[vmem] * 3,
        scratch_shapes=[
            pltpu.VMEM((breadth, B, 2 * B), f32),
            dma(()),
            dma((height,)),
            dma((height,)),
            dma(()),
            dma((height,)),
            dma((height,)),
            dma((breadth,)),
            dma((breadth,)),
            dma((breadth,)),
            dma((breadth,)),
        ],
        compiler_params=pltpu.CompilerParams(collective_id=0, has_side_effects=True),
        name="spread",
    )(own)


def vectors_kernel(height, breadth, stats, pc, pr, vc, vr, factor_ref, turned_ref, halves):
    first, second, factor, turned = factor_values(stats[:, :B], stats[:, B:].T)
    factor_ref[...] = factor
    turned_ref[...] = turned
    width = pc.shape[2]
    slots = lax.broadcasted_iota(jnp.int32, (B, width), 0)
    positions = lax.broadcasted_iota(jnp.int32, (B, width), 1)
    for pieces, out, base, count in (
        (pc, vc, lax.axis_index("col") * height, height),
        (pr, vr, lax.axis_index("row") * breadth, breadth),
    ):
        for i in range(count):
            start = (base + i) * width - B
            onehot = jnp.where(positions + start == slots, f32(1.0), f32(0.0))
            out[:, i * width : (i + 1) * width] = product(first, pieces[i]) - product(
                second, onehot
            )
    upper, lower = split(vc[...])
    halves[:B, :] = upper
    halves[B:, :] = lower


def vectors_of(stats, pc, pr, height, breadth):
    width = pc.shape[2]
    vmem = pl.BlockSpec(memory_space=pltpu.VMEM)
    return pl.pallas_call(
        lambda *refs: vectors_kernel(height, breadth, *refs),
        out_shape=[
            jax.ShapeDtypeStruct((B, height * width), f32),
            jax.ShapeDtypeStruct((B, breadth * width), f32),
            jax.ShapeDtypeStruct((B, B), f32),
            jax.ShapeDtypeStruct((B, B), f32),
            jax.ShapeDtypeStruct((2 * B, height * width), bf16),
        ],
        in_specs=[vmem] * 3,
        out_specs=[vmem] * 5,
        name="vectors",
    )(stats, pc, pr)


def image_kernel(
    height, breadth, z, vc, wc, wr, projected, rs, ex,
    rs_sends, rs_recvs, line_sems, wr_sems, role_sem, plane_sems, wc_sems, ex_sends, ex_recvs,
):
    me_row, me_col = lax.axis_index("row"), lax.axis_index("col")
    width = z.shape[2]
    in_plane = lambda other: (other, me_col)
    in_line = lambda other: (me_row, other)
    chunk = me_row * breadth + me_col
    to_row = lax.rem(chunk, height)
    to_col = chunk // height
    itself = jnp.logical_and(to_row == me_row, to_col == me_col)

    greet_all(height, breadth, me_row, me_col)

    def part_copy(step):
        other = lax.rem(me_col + step, breadth)
        return remote(
            z.at[other], rs.at[me_col], rs_sends.at[step], rs_recvs.at[me_col], in_line(other)
        )

    for step in range(1, breadth):
        part_copy(step).start()
    rs[me_col] = z[me_col]
    gather_received(rs, me_col, breadth, in_line, rs_sends, rs_recvs)
    total = rs[0]
    for k in range(1, breadth):
        total = total + rs[k]
    wr[me_col] = total
    role = remote(wr.at[me_col], wc.at[to_row], role_sem, wc_sems.at[to_row], (to_row, to_col))

    @pl.when(jnp.logical_not(itself))
    def _():
        role.start()

    gather_axis(wr, me_col, breadth, in_line, line_sems, wr_sems)

    @pl.when(itself)
    def _():
        wc[me_row] = total

    @pl.when(jnp.logical_not(itself))
    def _():
        remote(
            wc.at[me_row], wc.at[me_row], plane_sems.at[0], wc_sems.at[me_row],
            (lax.rem(me_row + 1, height), me_col),
        ).wait_recv()

    pair_gather(wc, me_row, height, in_plane, plane_sems, wc_sems)
    partial = jnp.zeros((B, B), f32)
    for i in range(height):
        partial = partial + product_nt(wc[i], vc[:, i * width : (i + 1) * width])
    ex[me_col] = jnp.concatenate([partial, jnp.zeros((B, B), f32)], axis=1)
    gather_axis(ex, me_col, breadth, in_line, ex_sends, ex_recvs)
    gather_received(ex, me_col, breadth, in_line, ex_sends, ex_recvs)
    summed = ex[0]
    for k in range(1, breadth):
        summed = summed + ex[k]
    projected[...] = summed
    gather_received(wr, me_col, breadth, in_line, line_sems, wr_sems)
    for step in range(1, breadth):
        part_copy(step).wait_send()

    @pl.when(jnp.logical_not(itself))
    def _():
        role.wait_send()

    gather_sent(wr, me_col, breadth, in_line, line_sems, wr_sems)
    pair_sent(wc, me_row, height, in_plane, plane_sems, wc_sems)
    gather_sent(ex, me_col, breadth, in_line, ex_sends, ex_recvs)


def images(z, vc, height, breadth):
    width = z.shape[2]
    vmem = pl.BlockSpec(memory_space=pltpu.VMEM)
    dma = pltpu.SemaphoreType.DMA
    return pl.pallas_call(
        lambda *refs: image_kernel(height, breadth, *refs),
        out_shape=[
            jax.ShapeDtypeStruct((height, B, width), f32),
            jax.ShapeDtypeStruct((breadth, B, width), f32),
            jax.ShapeDtypeStruct((B, 2 * B), f32),
        ],
        in_specs=[vmem] * 2,
        out_specs=[vmem] * 3,
        scratch_shapes=[
            pltpu.VMEM((breadth, B, width), f32),
            pltpu.VMEM((breadth, B, 2 * B), f32),
            dma((breadth,)),
            dma((breadth,)),
            dma((breadth,)),
            dma((breadth,)),
            dma(()),
            dma((height,)),
            dma((height,)),
            dma((breadth,)),
            dma((breadth,)),
        ],
        compiler_params=pltpu.CompilerParams(collective_id=1, has_side_effects=True),
        name="images",
    )(z, vc)


def image_part_kernel(block, halves, out):
    nt = (((1,), (1,)), ((), ()))
    rows, cols = block.shape
    size = min(512, cols)
    both = jnp.zeros((rows, 2 * B), f32)
    for start in range(0, cols, size):
        part = slice(start, start + size)
        upper, lower = split(block[:, part])
        both = both + lax.dot_general(upper, halves[:, part], nt, preferred_element_type=f32)
        low = lax.dot_general(lower, halves[:, part], nt, preferred_element_type=f32)
        both = both + jnp.where(lax.broadcasted_iota(jnp.int32, both.shape, 1) < B, low, f32(0.0))
    turned = both.T
    out[0] = turned[:B, :] + turned[B:, :]


def image_part(matrix, halves, width):
    rows, cols = matrix.shape
    return pl.pallas_call(
        image_part_kernel,
        grid=(rows // width,),
        out_shape=jax.ShapeDtypeStruct((rows // width, B, width), f32),
        in_specs=[
            pl.BlockSpec((width, cols), lambda i: (i, 0)),
            pl.BlockSpec((2 * B, cols), lambda i: (0, 0)),
        ],
        out_specs=pl.BlockSpec((1, B, width), lambda i: (i, 0, 0)),
        name="image_part",
    )(matrix, halves)


def final_kernel(block, left, right, out):
    cols = block.shape[1]
    size = min(512, cols)
    for start in range(0, cols, size):
        part = slice(start, start + size)
        out[:, part] = block[:, part] - jnp.dot(
            left[...], right[:, part], preferred_element_type=f32
        )


def final(matrix, left, right):
    rows, cols = matrix.shape
    tile = min(512, rows)
    depth = left.shape[1]
    return pl.pallas_call(
        final_kernel,
        grid=(rows // tile,),
        out_shape=jax.ShapeDtypeStruct((rows, cols), f32),
        in_specs=[
            pl.BlockSpec((tile, cols), lambda i: (i, 0)),
            pl.BlockSpec((tile, depth), lambda i: (i, 0)),
            pl.BlockSpec((depth, cols), lambda i: (0, 0)),
        ],
        out_specs=pl.BlockSpec((tile, cols), lambda i: (i, 0)),
        name="final",
    )(matrix, left, right)


def updates_kernel(height, breadth, projected, factor, turned, vc, vr, wc, wr, left, right):
    inner = product(turned[...], product(projected[:, :B], factor[...]))
    mix = jnp.concatenate([turned[...], -0.5 * inner], axis=1)
    width = wc.shape[2]
    for i in range(height):
        part = slice(i * width, (i + 1) * width)
        v = vc[:, part]
        u = product(mix, jnp.concatenate([wc[i], v], axis=0))
        upper, lower = split(jnp.concatenate([u, v], axis=0))
        right[: 2 * B, part] = upper
        right[2 * B : 4 * B, part] = upper
        right[4 * B :, part] = lower
    for i in range(breadth):
        part = slice(i * width, (i + 1) * width)
        v = vr[:, part]
        u = product(mix, jnp.concatenate([wr[i], v], axis=0))
        upper, lower = split(jnp.concatenate([v, u], axis=0).T)
        left[part, : 2 * B] = upper
        left[part, 2 * B : 4 * B] = lower
        left[part, 4 * B :] = upper


def updates(projected, factor, turned, vc, vr, wc, wr):
    height, breadth = wc.shape[0], wr.shape[0]
    vmem = pl.BlockSpec(memory_space=pltpu.VMEM)
    return pl.pallas_call(
        lambda *refs: updates_kernel(height, breadth, *refs),
        out_shape=[
            jax.ShapeDtypeStruct((vr.shape[1], 6 * B), bf16),
            jax.ShapeDtypeStruct((6 * B, vc.shape[1]), bf16),
        ],
        in_specs=[vmem] * 7,
        out_specs=[vmem] * 2,
        name="updates",
    )(projected, factor, turned, vc, vr, wc, wr)


def shards(height, breadth, matrix):
    rows, cols = matrix.shape
    width = cols // height
    global_cols = lax.axis_index("col") * cols + jnp.arange(cols, dtype=jnp.int32)
    masked = jnp.where(global_cols[None, :] >= B, matrix[0:B, :], f32(0.0))
    own = masked.reshape(B, height, width).transpose(1, 0, 2)
    pc, pr, stats = spread(own, height, breadth)
    vc, vr, factor, turned, halves = vectors_of(stats, pc, pr, height, breadth)
    z = image_part(matrix, halves, width)
    wc, wr, projected = images(z, vc, height, breadth)
    left, right = updates(projected, factor, turned, vc, vr, wc, wr)
    return final(matrix, left, right)


def solution(mesh):
    placed = (P("row", "col"),)
    height, breadth = mesh.shape["row"], mesh.shape["col"]
    return jax.shard_map(
        lambda matrix: shards(height, breadth, matrix),
        mesh=mesh,
        in_specs=placed,
        out_specs=P("row", "col"),
        check_vma=False,
    )
```
